768 devices in a mesh: section: 12 (over z_lo, core), tp: 16 (over z_hi, y), dp: 4 (over x).
Axes of the slice: x: 4, y: 8, z: 12 (z_hi: 2, z_lo: 6; z = z_hi * 6 + z_lo), core: 2. Of those that a mesh axis runs over, the one named last changes fastest.
Arguments:
- attn_out: bfloat16 [12, 1024, 8192], P('section', 'dp', 'tp'), may hold values from -6 to 6
- dest: int32 [1024, 1], P('dp'), may hold values from 0 to 3; in each aligned block of 256 rows (0 to 255, 256 to 511, ...) at most 128 rows name the same one
- o_weight: bfloat16 [12, 8192, 8192], P('section', 'tp'), may hold values from -0.0625 to 0.0625
- head: bfloat16 [12, 8192], P('section'), may hold values from -0.0625 to 0.0625
- coef: float32 [12], P('section'), may hold values from 0.5 to 1.5
Outputs:
- advantage: float32 [1024], P('dp')
The draws below stay inside these ranges and needn't reach their ends.
Inputs may be any that keep to these rules, and one draw needn't show every extreme that they name: `dest`: among the tokens of one index of dp, at most 128 have one value; every value 0 to 3 occurs among all 1024 tokens.
All inputs are finite; a program needn't handle non-finite values.
Results may differ from the reference program's by a relative error of at most 0.0003.
Values sent between devices are 32-bit elements; how exact they have to be, the bound alone decides.
No kernel may reach another device: no remote copies, remote signals or barrier semaphores. Data moves between devices by JAX's collectives and lax.ppermute only.
A program may use at most 64 MiB of HBM per device.

```python
import math
import jax
import jax.numpy as jnp
import numpy as np
from jax import lax

D = 8192
HD = 8192
TOK_DEV = 256
CAP = 128
TOKENS = 1024
SECTIONS = 12
N_DP = 4


def steps_of(stream_key, dims, shards, smallest, high):
    def one(dim, blocks):
        draws = jax.random.uniform(jax.random.fold_in(jax.random.fold_in(stream_key, 6), dim), (blocks,), jnp.float32, smallest / len(shards), high / len(shards))
        return jnp.repeat(jnp.exp(draws), dims[dim] // blocks).reshape((-1,) + (1,) * (len(dims) - dim - 1))

    loudness = one(*shards[0])
    for cut in shards[1:]:
        loudness = loudness * one(*cut)
    return loudness


def shared_out(own_key, own, number, rows, amount, top, most, lean):
    sequence = jax.random.permutation(own_key, amount)
    heavy_load, ordinary = load_shares(amount, rows * top, most, lean, True), load_shares(amount, rows * top, most, lean, False)
    places = jnp.arange(amount)

    def named(tallies, offset_by):
        used = int((tallies > 0).sum())
        fixed = max(1, used // 4)
        passed = fixed + (places - fixed + offset_by * (used - fixed)) % max(1, amount - fixed)
        return jnp.zeros((amount,), jnp.int32).at[sequence[jnp.where(places < fixed, places, passed)]].set(jnp.asarray(tallies, jnp.int32))

    tallies = jnp.where(number % 4 == 0, named(heavy_load, number // 4), named(ordinary, number - number // 4 - 1))
    mixed = jax.random.permutation(jax.random.fold_in(own, 3), amount)
    source_of, sink = mixed[0:amount // 2 * 2:2], mixed[1:amount // 2 * 2:2]
    margin = jnp.minimum(tallies[source_of] - 1, most - tallies[sink]) // 2
    margin = jnp.where((source_of == sequence[0]) | (sink == sequence[0]) | (tallies[sink] == 0), 0, jnp.maximum(margin, 0))
    passed = jax.random.randint(jax.random.fold_in(own, 4), (amount // 2,), 0, 1 << 20) % (margin + 1)
    tallies = tallies.at[source_of].add(-passed).at[sink].add(passed)
    labels = jnp.searchsorted(jnp.cumsum(tallies), jnp.arange(rows * top), side="right").astype(jnp.int32)
    listing = labels.reshape(top, rows).T
    listing = listing[jax.random.permutation(jax.random.fold_in(own, 1), rows)]
    offset_by = jax.random.randint(jax.random.fold_in(own, 2), (rows, 1), 0, top)
    return jnp.take_along_axis(listing, (jnp.arange(top)[None, :] + offset_by) % top, axis=1)


def load_shares(number_of, total, most, skew, full):
    portions = [(1 << 20) // math.isqrt(grade ** skew) + 1 for grade in range(1, number_of + 1)]
    largest = most if full else min(most, max(-(-total // number_of), total * portions[0] // sum(portions)))
    least = 1 if total - largest >= number_of - 1 else 0
    counts, rest = [largest] + [least] * (number_of - 1), total - largest - least * (number_of - 1)
    while rest > 0:
        movable = [i for i in range(1, number_of) if counts[i] < largest] or [i for i in range(1, number_of) if counts[i] < most]
        mass, left = sum([portions[i] for i in movable]), rest
        for i in movable:
            addition = min(most - counts[i], max(1, left * portions[i] // mass), rest)
            counts[i] = counts[i] + addition
            rest = rest - addition
    return np.array(counts)


def bell_draw(own_key, shape, spread, reach, split=(), kind=jnp.bfloat16):
    drawn = jax.random.normal(own_key, shape, jnp.float32) * spread
    if len(split) > 0:
        drawn = steps_of(own_key, shape, split, -0.22, 0.18) * drawn
    return jnp.clip(drawn, min=-reach, max=reach).astype(kind)


def setup_inputs(seed: int = 0) -> dict:
    arg_keys = jax.random.split(jax.random.key(seed), 6)
    attn_out = bell_draw(arg_keys[0], (SECTIONS, TOKENS, HD), 1.0, 6.0, ((0, 12), (1, 4), (2, 16)))
    dest_keys = jax.random.split(jax.random.fold_in(arg_keys[1], 1), TOKENS // TOK_DEV)
    dest_turns = jax.random.permutation(jax.random.fold_in(arg_keys[1], 3), TOKENS // TOK_DEV)
    dest = jax.vmap(lambda own, number: shared_out(jax.random.fold_in(arg_keys[1], 2), own, number, TOK_DEV, N_DP, 1, CAP, 2))(dest_keys, dest_turns).reshape((TOKENS, 1))
    o_weight = bell_draw(arg_keys[2], (SECTIONS, HD, D), HD ** -0.5, 0.0625, ((0, 12), (1, 16)))
    head = bell_draw(arg_keys[3], (SECTIONS, D), D ** -0.5, 0.0625, ((0, 12),))
    coef = jnp.clip(0.5 + 1.0 * jax.random.uniform(arg_keys[4], (SECTIONS,), jnp.float32) ** steps_of(arg_keys[4], (SECTIONS,), ((0, 12),), -0.2, 0.2), 0.5, 1.5)
    return dict(attn_out=attn_out, dest=dest, o_weight=o_weight, head=head, coef=coef)


def section_score(operands):
    features, matrix, head_row = operands
    projected = jnp.dot(features, matrix, preferred_element_type=jnp.float32)
    inverse_rms = lax.rsqrt(lax.optimization_barrier(jnp.mean(projected * projected, axis=1)) + 1e-05)
    return jnp.dot(projected, head_row.astype(jnp.float32), precision=lax.Precision.HIGHEST) * inverse_rms

def reference(attn_out, dest, o_weight, head, coef):
    section_scores = lax.map(section_score, (attn_out, o_weight, head))
    combined = lax.optimization_barrier(jnp.sum(section_scores * coef[:, None], axis=0))
    target = dest[:, 0]
    member_weight = (target[:, None] == jnp.arange(N_DP, dtype=jnp.int32)[None, :]).astype(jnp.float32)
    group_total = lax.optimization_barrier(jnp.sum(member_weight * combined[:, None], axis=0))
    group_count = lax.optimization_barrier(jnp.sum(member_weight, axis=0))
    group_mean = group_total / group_count
    return combined - lax.optimization_barrier(jnp.sum(member_weight * group_mean[None, :], axis=1))
```

```python
import jax
import jax.numpy as jnp
from jax import lax
from jax.sharding import Mesh, PartitionSpec as P


ZH = 2
SPLITS = (3072, 5120)


def body(attn_out, dest, o_weight, head, coef):
    rows = attn_out[0]
    matrix = o_weight[0]
    tokens, width = rows.shape[0], matrix.shape[1]
    zh, y, dp = lax.axis_index("zh"), lax.axis_index("y"), lax.axis_index("dp")
    ring, groups = lax.axis_size("y"), lax.axis_size("dp")
    own = tokens // (ring * ZH)
    swap = [(i, (i + 1) % ZH) for i in range(ZH)]

    squares, numer, start = 0.0, 0.0, 0
    for columns in SPLITS:
        partial_value = jnp.dot(
            rows, lax.slice_in_dim(matrix, start, start + columns, axis=1), preferred_element_type=jnp.float32
        )
        mine = lax.psum_scatter(partial_value, "y", scatter_dimension=0, tiled=True)
        low, high = mine[:own], mine[own:]
        kept = jnp.where(zh == 0, low, high)
        given = jnp.where(zh == 0, high, low)
        full = kept + lax.ppermute(given, "zh", swap)
        gain = head[0, start : start + columns].astype(jnp.float32)
        squares = squares + jnp.sum(full * full, axis=1)
        numer = numer + jnp.sum(full * gain[None, :], axis=1)
        start += columns
    score = coef[0] * numer * lax.rsqrt(squares / width + 1e-05)

    names = jnp.arange(groups, dtype=jnp.int32)[None, :]
    first = (y * ZH + zh) * own
    target = dest[:, 0]
    own_member = (lax.dynamic_slice_in_dim(target, first, own)[:, None] == names).astype(jnp.float32)
    totals = jnp.sum(own_member * score[:, None], axis=0)
    counts = jnp.where(lax.axis_index("section") == 0, jnp.sum(own_member, axis=0), 0.0)
    slots = lax.dynamic_update_slice(jnp.zeros((groups * tokens,), jnp.float32), score, (dp * tokens + first,))
    summed = lax.psum(jnp.concatenate([slots, totals, counts]), ("section", "zh", "y", "dp"))
    combined = lax.dynamic_slice_in_dim(summed, dp * tokens, tokens)
    tail = summed[groups * tokens :]
    group_mean = tail[:groups] / tail[groups:]
    member = (target[:, None] == names).astype(jnp.float32)
    return combined - jnp.sum(member * group_mean[None, :], axis=1)


def solution(mesh):
    sizes = mesh.shape
    split = Mesh(
        mesh.devices.reshape(sizes["section"], ZH, sizes["tp"] // ZH, sizes["dp"]), ("section", "zh", "y", "dp")
    )
    features = ("zh", "y")
    placed = (
        P("section", "dp", features),
        P("dp", None),
        P("section", features, None),
        P("section", None),
        P("section"),
    )
    return jax.shard_map(body, mesh=split, in_specs=placed, out_specs=P("dp"), check_vma=False)
```

```python
import jax
import jax.numpy as jnp
from jax import lax
from jax.sharding import Mesh, PartitionSpec as P


ZH = 2
Z_FIRST = 2304
LANES = 128


def everyone(value, axes):
    members = lax.axis_size(axes)
    padded = jnp.pad(value, (0, LANES - value.shape[0]))
    copies = jnp.broadcast_to(padded[None, :], (members, LANES))
    return lax.all_to_all(copies, axes, 0, 0, tiled=True)


def body(attn_out, dest, o_weight, head, coef):
    rows = attn_out[0]
    matrix = o_weight[0]
    tokens, width = rows.shape[0], matrix.shape[1]
    zh, y = lax.axis_index("zh"), lax.axis_index("y")
    ring, groups = lax.axis_size("y"), lax.axis_size("dp")
    own = tokens // (ring * ZH)
    swap = [(i, (i + 1) % ZH) for i in range(ZH)]
    cut = width - Z_FIRST

    def sides(value, axis):
        low, high = lax.index_in_dim(value, 0, axis, False), lax.index_in_dim(value, 1, axis, False)
        return jnp.where(zh == 0, low, high), jnp.where(zh == 0, high, low)

    y_first = jnp.dot(rows, matrix[:, :cut], preferred_element_type=jnp.float32)
    later_rows, y_first = lax.optimization_barrier((rows, y_first))
    z_first = jnp.dot(later_rows, matrix[:, cut:], preferred_element_type=jnp.float32)
    kept, given = sides(z_first.reshape(ring, ZH, own, Z_FIRST), 1)
    z_summed = kept + lax.ppermute(given, "zh", swap)

    part = lax.psum_scatter(y_first, "y", scatter_dimension=0, tiled=True)
    kept, given = sides(part.reshape(ZH, own, cut), 0)
    given, z_summed = lax.optimization_barrier((given, z_summed))
    second = lax.psum_scatter(z_summed.reshape(ring * own, Z_FIRST), "y", scatter_dimension=0, tiled=True)
    first = kept + lax.ppermute(given, "zh", swap)

    gain = head[0].astype(jnp.float32)
    squares = jnp.sum(first * first, axis=1) + jnp.sum(second * second, axis=1)
    numer = jnp.sum(first * gain[None, :cut], axis=1) + jnp.sum(second * gain[None, cut:], axis=1)
    score = coef[0] * numer * lax.rsqrt(squares / width + 1e-05)

    names = jnp.arange(groups, dtype=jnp.int32)[None, :]
    target = dest[:, 0]
    own_target = lax.dynamic_slice_in_dim(target, (y * ZH + zh) * own, own)
    own_member = (own_target[:, None] == names).astype(jnp.float32)
    combined = jnp.sum(everyone(score, "section"), axis=0)[:own]
    totals = jnp.sum(own_member * combined[:, None], axis=0)
    counts = jnp.sum(own_member, axis=0)
    pieces = everyone(jnp.concatenate([combined, totals, counts]), ("dp", "y", "zh"))
    pieces = pieces.reshape(groups, ring * ZH, LANES)
    mine = lax.dynamic_index_in_dim(pieces, lax.axis_index("dp"), 0, False)[:, :own].reshape(tokens)
    tail = jnp.sum(pieces[:, :, own : own + 2 * groups], axis=(0, 1))
    group_mean = tail[:groups] / tail[groups:]
    member = (target[:, None] == names).astype(jnp.float32)
    return mine - jnp.sum(member * group_mean[None, :], axis=1)


def solution(mesh):
    sizes = mesh.shape
    split = Mesh(
        mesh.devices.reshape(sizes["section"], ZH, sizes["tp"] // ZH, sizes["dp"]), ("section", "zh", "y", "dp")
    )
    features = ("zh", "y")
    placed = (
        P("section", "dp", features),
        P("dp", None),
        P("section", features, None),
        P("section", None),
        P("section"),
    )
    return jax.shard_map(body, mesh=split, in_specs=placed, out_specs=P("dp"), check_vma=False)
```

```python
import jax
import jax.numpy as jnp
from jax import lax
from jax.sharding import Mesh, PartitionSpec as P


ZH = 2
SPLITS = (4096, 4096)
LANES = 128


def everyone(value, axes):
    members = lax.axis_size(axes)
    padded = jnp.pad(value, (0, LANES - value.shape[0]))
    copies = jnp.broadcast_to(padded[None, :], (members, LANES))
    return lax.all_to_all(copies, axes, 0, 0, tiled=True)


def body(attn_out, dest, o_weight, head, coef):
    rows = attn_out[0]
    matrix = o_weight[0]
    tokens, width = rows.shape[0], matrix.shape[1]
    zh, y = lax.axis_index("zh"), lax.axis_index("y")
    ring, groups = lax.axis_size("y"), lax.axis_size("dp")
    own = tokens // (ring * ZH)
    far = ring // 2
    swap = [(i, (i + 1) % ZH) for i in range(ZH)]

    sent = []

    def join(*values):
        total = values[0]
        for value in values[1:]:
            total = total + value
        return total

    def ship(value, axis, pairs):
        sent.append(value)
        return lax.ppermute(value, axis, pairs)

    def along(value, by):
        return ship(value, "y", [(i, (i + by) % ring) for i in range(ring)])

    def after_last(value):
        return lax.optimization_barrier((value, sent[-1]))[0] if sent else value

    cuts = [0]
    for columns in SPLITS:
        cuts.append(cuts[-1] + columns)
    spans = range(len(SPLITS))
    parts, ups, downs = [], [], []

    def owned_by(g, owner):
        return lax.dynamic_index_in_dim(parts[g], owner % ring, 0, False)

    for g in spans:
        product = jnp.dot(after_last(rows), matrix[:, cuts[g] : cuts[g + 1]], preferred_element_type=jnp.float32)
        parts.append(product.reshape(ring, ZH, own, SPLITS[g]))
        opposite = owned_by(g, y + far)
        ups.append(along(opposite[0], 1)[None])
        downs.append(along(opposite[1], -1)[None])
    for step in range(far - 1, 0, -1):
        for g in spans:
            up = after_last(ups[g])
            if step == far - 1:
                up = lax.pad(up, 0.0, ((0, 1, 0), (0, 0, 0), (0, 0, 0)))
            ups[g] = along(join(owned_by(g, y + step), up), 1)
            down = after_last(downs[g])
            if step == far - 1:
                down = lax.pad(down, 0.0, ((1, 0, 0), (0, 0, 0), (0, 0, 0)))
            downs[g] = along(join(owned_by(g, y - step), down), -1)

    gain = head[0].astype(jnp.float32)
    squares, numer = 0.0, 0.0
    for g in spans:
        total = join(owned_by(g, y), after_last(ups[g]), downs[g])
        kept = jnp.where(zh == 0, total[0], total[1])
        given = jnp.where(zh == 0, total[1], total[0])
        full = kept + ship(given, "zh", swap)
        squares = squares + jnp.sum(full * full, axis=1)
        numer = numer + jnp.sum(full * gain[None, cuts[g] : cuts[g + 1]], axis=1)
    score = coef[0] * numer * lax.rsqrt(squares / width + 1e-05)

    names = jnp.arange(groups, dtype=jnp.int32)[None, :]
    target = dest[:, 0]
    own_target = lax.dynamic_slice_in_dim(target, (y * ZH + zh) * own, own)
    own_member = (own_target[:, None] == names).astype(jnp.float32)
    combined = jnp.sum(everyone(score, "section"), axis=0)[:own]
    totals = jnp.sum(own_member * combined[:, None], axis=0)
    counts = jnp.sum(own_member, axis=0)
    pieces = everyone(jnp.concatenate([combined, totals, counts]), ("dp", "y", "zh"))
    pieces = pieces.reshape(groups, ring * ZH, LANES)
    mine = lax.dynamic_index_in_dim(pieces, lax.axis_index("dp"), 0, False)[:, :own].reshape(tokens)
    tail = jnp.sum(pieces[:, :, own : own + 2 * groups], axis=(0, 1))
    group_mean = tail[:groups] / tail[groups:]
    member = (target[:, None] == names).astype(jnp.float32)
    return mine - jnp.sum(member * group_mean[None, :], axis=1)


def solution(mesh):
    sizes = mesh.shape
    split = Mesh(
        mesh.devices.reshape(sizes["section"], ZH, sizes["tp"] // ZH, sizes["dp"]), ("section", "zh", "y", "dp")
    )
    features = ("zh", "y")
    placed = (
        P("section", "dp", features),
        P("dp", None),
        P("section", features, None),
        P("section", None),
        P("section"),
    )

    return jax.shard_map(body, mesh=split, in_specs=placed, out_specs=P("dp"), check_vma=False)
```

```python
import jax
import jax.numpy as jnp
from jax import lax
from jax.sharding import Mesh, PartitionSpec as P


ZH = 2
SPLITS = (3584, 3328)
Z_FIRST = 1280
LANES = 128


def everyone(value, axes):
    members = lax.axis_size(axes)
    padded = jnp.pad(value, (0, LANES - value.shape[0]))
    copies = jnp.broadcast_to(padded[None, :], (members, LANES))
    return lax.all_to_all(copies, axes, 0, 0, tiled=True)


def body(attn_out, dest, o_weight, head, coef):
    rows = attn_out[0]
    matrix = o_weight[0]
    tokens, width = rows.shape[0], matrix.shape[1]
    zh, y = lax.axis_index("zh"), lax.axis_index("y")
    ring, groups = lax.axis_size("y"), lax.axis_size("dp")
    own = tokens // (ring * ZH)
    far = ring // 2
    swap = [(i, (i + 1) % ZH) for i in range(ZH)]

    sent = []

    def join(*values):
        total = values[0]
        for value in values[1:]:
            total = total + value
        return total

    def ship(value, axis, pairs):
        sent.append(value)
        return lax.ppermute(value, axis, pairs)

    def along(value, by):
        return ship(value, "y", [(i, (i + by) % ring) for i in range(ring)])

    def after_last(value):
        return lax.optimization_barrier((value, sent[-1]))[0] if sent else value

    cuts = [0]
    for columns in SPLITS:
        cuts.append(cuts[-1] + columns)
    spans = range(len(SPLITS))
    parts, ups, downs = [], [], []

    def owned_by(g, owner):
        return lax.dynamic_index_in_dim(parts[g], owner % ring, 0, False)

    for g in spans:
        product = jnp.dot(after_last(rows), matrix[:, cuts[g] : cuts[g + 1]], preferred_element_type=jnp.float32)
        parts.append(product.reshape(ring, ZH, own, SPLITS[g]))
        opposite = owned_by(g, y + far)
        ups.append(along(opposite[0], 1)[None])
        downs.append(along(opposite[1], -1)[None])

    def z_sides(value):
        return jnp.where(zh == 0, value[:, 0], value[:, 1]), jnp.where(zh == 0, value[:, 1], value[:, 0])

    for step in range(far - 1, 0, -1):
        for g in spans:
            if step == far - 1 and g == 1:
                product = jnp.dot(after_last(rows), matrix[:, cuts[-1] :], preferred_element_type=jnp.float32)
                kept, given = z_sides(product.reshape(ring, ZH, own, Z_FIRST))
                received = ship(given, "zh", swap)
                z_summed = kept + received
            up = after_last(ups[g])
            if step == far - 1:
                up = lax.pad(up, 0.0, ((0, 1, 0), (0, 0, 0), (0, 0, 0)))
            ups[g] = along(join(owned_by(g, y + step), up), 1)
            down = after_last(downs[g])
            if step == far - 1:
                down = lax.pad(down, 0.0, ((1, 0, 0), (0, 0, 0), (0, 0, 0)))
            downs[g] = along(join(owned_by(g, y - step), down), -1)

    gain = head[0].astype(jnp.float32)
    squares, numer = 0.0, 0.0

    def measured(full, first, last):
        return jnp.sum(full * full, axis=1), jnp.sum(full * gain[None, first:last], axis=1)

    done = []
    for g in spans:
        total = join(owned_by(g, y), after_last(ups[g]), downs[g])
        kept = jnp.where(zh == 0, total[0], total[1])
        given = jnp.where(zh == 0, total[1], total[0])
        done.append((kept + ship(given, "zh", swap), cuts[g], cuts[g + 1]))
        if g == 0:
            sent.append(given)
            turned = lax.all_to_all(z_summed, "y", 0, 0, tiled=True)
    done.append((jnp.sum(turned, axis=0), cuts[-1], width))
    for full, first, last in done:
        square, product = measured(full, first, last)
        squares, numer = squares + square, numer + product
    score = coef[0] * numer * lax.rsqrt(squares / width + 1e-05)

    names = jnp.arange(groups, dtype=jnp.int32)[None, :]
    target = dest[:, 0]
    pair = ZH * own
    pair_target = lax.dynamic_slice_in_dim(target, y * pair, pair)
    pair_member = (pair_target[:, None] == names).astype(jnp.float32)
    scores = everyone(score, ("zh", "section")).reshape(ZH, -1, LANES)
    combined = jnp.sum(scores, axis=1)[:, :own].reshape(pair)
    totals = jnp.sum(pair_member * combined[:, None], axis=0)
    counts = jnp.sum(pair_member, axis=0)
    pieces = everyone(jnp.concatenate([combined, totals, counts]), ("dp", "y")).reshape(groups, ring, LANES)
    mine = lax.dynamic_index_in_dim(pieces, lax.axis_index("dp"), 0, False)[:, :pair].reshape(tokens)
    tail = jnp.sum(pieces[:, :, pair : pair + 2 * groups], axis=(0, 1))
    group_mean = tail[:groups] / tail[groups:]
    member = (target[:, None] == names).astype(jnp.float32)
    return mine - jnp.sum(member * group_mean[None, :], axis=1)


def solution(mesh):
    sizes = mesh.shape
    split = Mesh(
        mesh.devices.reshape(sizes["section"], ZH, sizes["tp"] // ZH, sizes["dp"]), ("section", "zh", "y", "dp")
    )
    features = ("zh", "y")
    placed = (
        P("section", "dp", features),
        P("dp", None),
        P("section", features, None),
        P("section", None),
        P("section"),
    )

    return jax.shard_map(body, mesh=split, in_specs=placed, out_specs=P("dp"), check_vma=False)
```

```python
import jax
import jax.numpy as jnp
from jax import lax
from jax.experimental import pallas as pl
from jax.experimental.pallas import tpu as pltpu
from jax.sharding import Mesh, PartitionSpec as P


ZH = 2
SPLITS = (3584, 3072)
Z_FIRST = 1536
BLOCK = 512
LANES = 128


def everyone(value, axes):
    members = lax.axis_size(axes)
    padded = jnp.pad(value, (0, LANES - value.shape[0]))
    copies = jnp.broadcast_to(padded[None, :], (members, LANES))
    return lax.all_to_all(copies, axes, 0, 0, tiled=True)


def products(rows, weights, place, ring, own):
    tokens, depth = rows.shape
    counts = [columns // BLOCK for columns in SPLITS]
    y_first, z_blocks = sum(counts), Z_FIRST // BLOCK

    def kernel(place_ref, rows_ref, w_ref, up_ref, down_ref, *rest):
        group_refs, (kept_ref, given_ref), held = rest[: len(counts)], rest[len(counts) : -1], rest[-1]
        block = pl.program_id(0)
        product = jnp.dot(rows_ref[...], w_ref[...], preferred_element_type=jnp.float32)
        start = 0
        for group_ref, count in zip(group_refs, counts):

            @pl.when((block >= start) & (block < start + count))
            def _(group_ref=group_ref):
                group_ref[...] = product

            start += count

        @pl.when(block < y_first)
        def _():
            held[...] = product
            first = pl.multiple_of(place_ref[0] * (ZH * own), ZH * own)
            up_ref[...] = held[pl.ds(first, own), :]
            down_ref[...] = held[pl.ds(pl.multiple_of(first + own, own), own), :]

        @pl.when(block >= y_first)
        def _():
            sides = product.reshape(ring, ZH, own, BLOCK)
            low, high = sides[:, 0], sides[:, 1]
            kept_ref[...] = jnp.where(place_ref[1] == 0, low, high)
            given_ref[...] = jnp.where(place_ref[1] == 0, high, low)

    def spec(height, first, count):
        return pl.BlockSpec((height, BLOCK), lambda j, p: (0, jnp.clip(j - first, 0, count - 1)))

    starts = [sum(counts[:g]) for g in range(len(counts))]
    z_spec = pl.BlockSpec((ring, own, BLOCK), lambda j, p: (0, 0, jnp.clip(j - y_first, 0, z_blocks - 1)))
    f32 = jnp.float32
    return pl.pallas_call(
        kernel,
        grid_spec=pltpu.PrefetchScalarGridSpec(
            num_scalar_prefetch=1,
            grid=(y_first + z_blocks,),
            in_specs=[
                pl.BlockSpec((tokens, depth), lambda j, p: (0, 0)),
                pl.BlockSpec((None, depth, BLOCK), lambda j, p: (0, 0, j)),
            ],
            out_specs=[spec(own, 0, y_first), spec(own, 0, y_first)]
            + [spec(tokens, first, count) for first, count in zip(starts, counts)]
            + [z_spec, z_spec],
            scratch_shapes=[pltpu.VMEM((tokens, BLOCK), f32)],
        ),
        out_shape=[jax.ShapeDtypeStruct((own, y_first * BLOCK), f32)] * 2
        + [jax.ShapeDtypeStruct((tokens, columns), f32) for columns in SPLITS]
        + [jax.ShapeDtypeStruct((ring, own, Z_FIRST), f32)] * 2,
    )(place, rows, weights)


def body(attn_out, dest, o_weight, head, coef):
    rows = attn_out[0]
    tokens, width = rows.shape[0], o_weight.shape[2]
    zh, y = lax.axis_index("zh"), lax.axis_index("y")
    ring, groups = lax.axis_size("y"), lax.axis_size("dp")
    own = tokens // (ring * ZH)
    far = ring // 2
    swap = [(i, (i + 1) % ZH) for i in range(ZH)]

    sent = []

    def join(*values):
        total = values[0]
        for value in values[1:]:
            total = total + value
        return total

    def ship(value, axis, pairs):
        sent.append(value)
        return lax.ppermute(value, axis, pairs)

    def along(value, by):
        return ship(value, "y", [(i, (i + by) % ring) for i in range(ring)])

    def after_last(value):
        return lax.optimization_barrier((value, sent[-1]))[0] if sent else value

    cuts = [0]
    for columns in SPLITS:
        cuts.append(cuts[-1] + columns)
    spans = range(len(SPLITS))

    def owned_by(g, owner):
        return lax.dynamic_index_in_dim(parts[g], owner % ring, 0, False)

    place = jnp.stack([(y + far) % ring, zh]).astype(jnp.int32)
    up_first, down_first, *parts, kept, given = products(rows, o_weight, place, ring, own)
    parts = [part.reshape(ring, ZH, own, part.shape[1]) for part in parts]
    ups = [along(up_first, 1)[None]] * len(SPLITS)
    downs = [along(down_first, -1)[None]] * len(SPLITS)
    received = ship(given, "zh", swap)
    z_summed = kept + received

    for step in range(far - 1, 0, -1):
        for g in spans:
            up = after_last(ups[g])
            if step == far - 1:
                up = lax.pad(up[:, :, cuts[g] : cuts[g + 1]], 0.0, ((0, 1, 0), (0, 0, 0), (0, 0, 0)))
            ups[g] = along(join(owned_by(g, y + step), up), 1)
            down = after_last(downs[g])
            if step == far - 1:
                down = lax.pad(down[:, :, cuts[g] : cuts[g + 1]], 0.0, ((1, 0, 0), (0, 0, 0), (0, 0, 0)))
            downs[g] = along(join(owned_by(g, y - step), down), -1)

    gain = head[0].astype(jnp.float32)
    squares, numer = 0.0, 0.0

    def measured(full, first, last):
        return jnp.sum(full * full, axis=1), jnp.sum(full * gain[None, first:last], axis=1)

    done = []
    for g in spans:
        total = join(owned_by(g, y), after_last(ups[g]), downs[g])
        kept = jnp.where(zh == 0, total[0], total[1])
        given = jnp.where(zh == 0, total[1], total[0])
        done.append((kept + ship(given, "zh", swap), cuts[g], cuts[g + 1]))
    turned = lax.all_to_all(z_summed, "y", 0, 0, tiled=True)
    done.append((jnp.sum(turned, axis=0), cuts[-1], width))
    for full, first, last in done:
        square, weighted = measured(full, first, last)
        squares, numer = squares + square, numer + weighted
    score = coef[0] * numer * lax.rsqrt(squares / width + 1e-05)

    names = jnp.arange(groups, dtype=jnp.int32)[None, :]
    target = dest[:, 0]
    pair = ZH * own
    pair_target = lax.dynamic_slice_in_dim(target, y * pair, pair)
    pair_member = (pair_target[:, None] == names).astype(jnp.float32)
    scores = everyone(score, ("zh", "section")).reshape(ZH, -1, LANES)
    combined = jnp.sum(scores, axis=1)[:, :own].reshape(pair)
    totals = jnp.sum(pair_member * combined[:, None], axis=0)
    counts = jnp.sum(pair_member, axis=0)
    pieces = everyone(jnp.concatenate([combined, totals, counts]), ("dp", "y")).reshape(groups, ring, LANES)
    mine = lax.dynamic_index_in_dim(pieces, lax.axis_index("dp"), 0, False)[:, :pair].reshape(tokens)
    tail = jnp.sum(pieces[:, :, pair : pair + 2 * groups], axis=(0, 1))
    group_mean = tail[:groups] / tail[groups:]
    member = (target[:, None] == names).astype(jnp.float32)
    return mine - jnp.sum(member * group_mean[None, :], axis=1)


def solution(mesh):
    sizes = mesh.shape
    split = Mesh(
        mesh.devices.reshape(sizes["section"], ZH, sizes["tp"] // ZH, sizes["dp"]), ("section", "zh", "y", "dp")
    )
    features = ("zh", "y")
    placed = (
        P("section", "dp", features),
        P("dp", None),
        P("section", features, None),
        P("section", None),
        P("section"),
    )

    return jax.shard_map(body, mesh=split, in_specs=placed, out_specs=P("dp"), check_vma=False)
```

```python
import jax
import jax.numpy as jnp
from jax import lax
from jax.sharding import Mesh, PartitionSpec as P


ZH = 2
SPLITS = (3584, 3328)
Z_FIRST = 1280
LANES = 128


def everyone(value, axes):
    members = lax.axis_size(axes)
    padded = jnp.pad(value, (0, LANES - value.shape[0]))
    copies = jnp.broadcast_to(padded[None, :], (members, LANES))
    return lax.all_to_all(copies, axes, 0, 0, tiled=True)


def body(attn_out, dest, o_weight, head, coef):
    rows = attn_out[0]
    matrix = o_weight[0]
    tokens, width = rows.shape[0], matrix.shape[1]
    zh, y = lax.axis_index("zh"), lax.axis_index("y")
    ring, groups = lax.axis_size("y"), lax.axis_size("dp")
    own = tokens // (ring * ZH)
    far = ring // 2
    swap = [(i, (i + 1) % ZH) for i in range(ZH)]

    sent = []

    def join(*values):
        total = values[0]
        for value in values[1:]:
            total = total + value
        return total

    def ship(value, axis, pairs):
        sent.append(value)
        return lax.ppermute(value, axis, pairs)

    def along(value, by):
        return ship(value, "y", [(i, (i + by) % ring) for i in range(ring)])

    def after_last(value):
        return lax.optimization_barrier((value, sent[-1]))[0] if sent else value

    cuts = [0]
    for columns in SPLITS:
        cuts.append(cuts[-1] + columns)
    spans = range(len(SPLITS))
    parts, ups, downs = [], [], []

    def owned_by(g, owner):
        return lax.dynamic_index_in_dim(parts[g], owner % ring, 0, False)

    columns = cuts[-1]
    opposite_rows = lax.dynamic_slice_in_dim(rows, (y + far) % ring * (ZH * own), ZH * own)
    opposite = jnp.dot(opposite_rows, matrix[:, :columns], preferred_element_type=jnp.float32)
    up_first = along(opposite[:own], 1)[None]
    down_first = along(opposite[own:], -1)[None]

    def group_product(g):
        product = jnp.dot(after_last(rows), matrix[:, cuts[g] : cuts[g + 1]], preferred_element_type=jnp.float32)
        parts.append(product.reshape(ring, ZH, own, SPLITS[g]))
        ups.append(up_first)
        downs.append(down_first)

    group_product(0)

    def z_sides(value):
        return jnp.where(zh == 0, value[:, 0], value[:, 1]), jnp.where(zh == 0, value[:, 1], value[:, 0])

    for step in range(far - 1, 0, -1):
        for g in spans:
            if step == far - 1 and g == 1:
                group_product(1)
                z_product = jnp.dot(after_last(rows), matrix[:, columns:], preferred_element_type=jnp.float32)
                kept, given = z_sides(z_product.reshape(ring, ZH, own, Z_FIRST))
                received = ship(given, "zh", swap)
                z_summed = kept + received
            up = after_last(ups[g])
            if step == far - 1:
                up = lax.pad(up[:, :, cuts[g] : cuts[g + 1]], 0.0, ((0, 1, 0), (0, 0, 0), (0, 0, 0)))
            ups[g] = along(join(owned_by(g, y + step), up), 1)
            down = after_last(downs[g])
            if step == far - 1:
                down = lax.pad(down[:, :, cuts[g] : cuts[g + 1]], 0.0, ((1, 0, 0), (0, 0, 0), (0, 0, 0)))
            downs[g] = along(join(owned_by(g, y - step), down), -1)

    gain = head[0].astype(jnp.float32)
    squares, numer = 0.0, 0.0

    def measured(full, first, last):
        return jnp.sum(full * full, axis=1), jnp.sum(full * gain[None, first:last], axis=1)

    done = []
    for g in spans:
        total = join(owned_by(g, y), after_last(ups[g]), downs[g])
        kept = jnp.where(zh == 0, total[0], total[1])
        given = jnp.where(zh == 0, total[1], total[0])
        done.append((kept + ship(given, "zh", swap), cuts[g], cuts[g + 1]))
    turned = lax.all_to_all(z_summed, "y", 0, 0, tiled=True)
    done.append((jnp.sum(turned, axis=0), cuts[-1], width))
    for full, first, last in done:
        square, weighted = measured(full, first, last)
        squares, numer = squares + square, numer + weighted
    score = coef[0] * numer * lax.rsqrt(squares / width + 1e-05)

    names = jnp.arange(groups, dtype=jnp.int32)[None, :]
    target = dest[:, 0]
    pair = ZH * own
    pair_target = lax.dynamic_slice_in_dim(target, y * pair, pair)
    pair_member = (pair_target[:, None] == names).astype(jnp.float32)
    scores = everyone(score, ("zh", "section")).reshape(ZH, -1, LANES)
    combined = jnp.sum(scores, axis=1)[:, :own].reshape(pair)
    totals = jnp.sum(pair_member * combined[:, None], axis=0)
    counts = jnp.sum(pair_member, axis=0)
    pieces = everyone(jnp.concatenate([combined, totals, counts]), ("dp", "y")).reshape(groups, ring, LANES)
    mine = lax.dynamic_index_in_dim(pieces, lax.axis_index("dp"), 0, False)[:, :pair].reshape(tokens)
    tail = jnp.sum(pieces[:, :, pair : pair + 2 * groups], axis=(0, 1))
    group_mean = tail[:groups] / tail[groups:]
    member = (target[:, None] == names).astype(jnp.float32)
    return mine - jnp.sum(member * group_mean[None, :], axis=1)


def solution(mesh):
    sizes = mesh.shape
    split = Mesh(
        mesh.devices.reshape(sizes["section"], ZH, sizes["tp"] // ZH, sizes["dp"]), ("section", "zh", "y", "dp")
    )
    features = ("zh", "y")
    placed = (
        P("section", "dp", features),
        P("dp", None),
        P("section", features, None),
        P("section", None),
        P("section"),
    )

    return jax.shard_map(body, mesh=split, in_specs=placed, out_specs=P("dp"), check_vma=False)
```

```python
import jax
import jax.numpy as jnp
from jax import lax
from jax.sharding import Mesh, PartitionSpec as P


ZH = 2
SPLITS = (3584, 3328)
Z_FIRST = 1280
LANES = 128


def everyone(value, axes):
    members = lax.axis_size(axes)
    padded = jnp.pad(value, (0, LANES - value.shape[0]))
    copies = jnp.broadcast_to(padded[None, :], (members, LANES))
    return lax.all_to_all(copies, axes, 0, 0, tiled=True)


def body(attn_out, dest, o_weight, head, coef):
    rows = attn_out[0]
    matrix = o_weight[0]
    tokens, width = rows.shape[0], matrix.shape[1]
    zh, y = lax.axis_index("zh"), lax.axis_index("y")
    ring, groups = lax.axis_size("y"), lax.axis_size("dp")
    own = tokens // (ring * ZH)
    far = ring // 2
    swap = [(i, (i + 1) % ZH) for i in range(ZH)]

    sent = []

    def join(*values):
        total = values[0]
        for value in values[1:]:
            total = total + value
        return total

    def ship(value, axis, pairs):
        sent.append(value)
        return lax.ppermute(value, axis, pairs)

    def along(value, by):
        return ship(value, "y", [(i, (i + by) % ring) for i in range(ring)])

    def after_last(value):
        return lax.optimization_barrier((value, sent[-1]))[0] if sent else value

    cuts = [0]
    for columns in SPLITS:
        cuts.append(cuts[-1] + columns)
    spans = range(len(SPLITS))
    parts, ups, downs = [], [], []

    def owned_by(g, owner):
        return lax.dynamic_index_in_dim(parts[g], owner % ring, 0, False)

    columns = cuts[-1]
    opposite_rows = lax.dynamic_slice_in_dim(rows, (y + far) % ring * (ZH * own), ZH * own)
    opposite = jnp.dot(opposite_rows, matrix[:, :columns], preferred_element_type=jnp.float32)
    up_first = along(opposite[:own], 1)[None]
    down_first = along(opposite[own:], -1)[None]

    def group_product(g):
        product = jnp.dot(after_last(rows), matrix[:, cuts[g] : cuts[g + 1]], preferred_element_type=jnp.float32)
        parts.append(product.reshape(ring, ZH, own, SPLITS[g]))
        ups.append(up_first)
        downs.append(down_first)

    group_product(0)

    def z_sides(value):
        return jnp.where(zh == 0, value[:, 0], value[:, 1]), jnp.where(zh == 0, value[:, 1], value[:, 0])

    for step in range(far - 1, 0, -1):
        for g in spans:
            if step == far - 1 and g == 1:
                group_product(1)
                z_product = jnp.dot(after_last(rows), matrix[:, columns:], preferred_element_type=jnp.float32)
                kept, given = z_sides(z_product.reshape(ring, ZH, own, Z_FIRST))
                received = ship(given, "zh", swap)
                z_summed = kept + received
            up = after_last(ups[g])
            if step == far - 1:
                up = lax.pad(up[:, :, cuts[g] : cuts[g + 1]], 0.0, ((0, 1, 0), (0, 0, 0), (0, 0, 0)))
            ups[g] = along(join(owned_by(g, y + step), up), 1)
            down = after_last(downs[g])
            if step == far - 1:
                down = lax.pad(down[:, :, cuts[g] : cuts[g + 1]], 0.0, ((1, 0, 0), (0, 0, 0), (0, 0, 0)))
            downs[g] = along(join(owned_by(g, y - step), down), -1)

    gain = head[0].astype(jnp.float32)
    squares, numer = 0.0, 0.0

    def measured(full, first, last):
        return jnp.sum(full * full, axis=1), jnp.sum(full * gain[None, first:last], axis=1)

    done = []
    for g in spans:
        total = join(owned_by(g, y), after_last(ups[g]), downs[g])
        kept = jnp.where(zh == 0, total[0], total[1])
        given = jnp.where(zh == 0, total[1], total[0])
        done.append((kept + ship(given, "zh", swap), cuts[g], cuts[g + 1]))
    turned = lax.all_to_all(z_summed, "y", 0, 0, tiled=True)
    done.append((jnp.sum(turned, axis=0), cuts[-1], width))
    for full, first, last in done:
        square, weighted = measured(full, first, last)
        squares, numer = squares + square, numer + weighted
    score = coef[0] * numer * lax.rsqrt(squares / width + 1e-05)

    names = jnp.arange(groups, dtype=jnp.int32)[None, :]
    target = dest[:, 0]
    pair = ZH * own
    pair_target = lax.dynamic_slice_in_dim(target, y * pair, pair)
    pair_member = (pair_target[:, None] == names).astype(jnp.float32)
    scores = everyone(score, ("zh", "section"))
    side = jnp.arange(scores.shape[0])[:, None] // (scores.shape[0] // ZH)
    combined = jnp.concatenate([jnp.sum(jnp.where(side == z, scores, 0.0), axis=0)[:own] for z in range(ZH)])
    totals = jnp.sum(pair_member * combined[:, None], axis=0)
    counts = jnp.sum(pair_member, axis=0)
    pieces = everyone(jnp.concatenate([combined, totals, counts]), ("dp", "y")).reshape(groups, ring, LANES)
    mine = lax.dynamic_index_in_dim(pieces, lax.axis_index("dp"), 0, False)[:, :pair].reshape(tokens)
    tail = jnp.sum(pieces[:, :, pair : pair + 2 * groups], axis=(0, 1))
    group_mean = tail[:groups] / tail[groups:]
    member = (target[:, None] == names).astype(jnp.float32)
    return mine - jnp.sum(member * group_mean[None, :], axis=1)


def solution(mesh):
    sizes = mesh.shape
    split = Mesh(
        mesh.devices.reshape(sizes["section"], ZH, sizes["tp"] // ZH, sizes["dp"]), ("section", "zh", "y", "dp")
    )
    features = ("zh", "y")
    placed = (
        P("section", "dp", features),
        P("dp", None),
        P("section", features, None),
        P("section", None),
        P("section"),
    )

    return jax.shard_map(body, mesh=split, in_specs=placed, out_specs=P("dp"), check_vma=False)
```
